256 devices in a mesh: rows: 64 (over z, y, x_hi), panel: 4 (over x_lo, core).
Axes of the slice: x: 4 (x_hi: 2, x_lo: 2; x = x_hi * 2 + x_lo), y: 4, z: 8, core: 2. Of those that a mesh axis runs over, the one named last changes fastest.
Arguments:
- acts: bfloat16 [262144, 4096], P('rows', 'panel'), may hold values from -16 to 16
- basis: bfloat16 [4096, 256], P('panel'), may hold values from -0.09375 to 0.09375
- center: float32 [4096], P('panel'), may hold values from -6 to 6
- mask: int32 [262144], P('rows'), may hold values 0 or 1
Outputs:
- orthonormal: float32 [4096, 256], P('panel')
- scores: bfloat16 [262144, 256], P(('rows', 'panel'))
- subset_mean: float32 [256], replicated
- subset_cov: float32 [256, 256], replicated
The draws below stay inside these ranges and needn't reach their ends.
Inputs may be any that keep to these rules, and one draw needn't show every extreme that they name: `mask`: 1 marks a row of the h-subset.
All inputs are finite; a program needn't handle non-finite values. No bound on the sum of `mask` on one device may be relied on, other than what follows from the above.
Results may differ from the reference program's by a relative error of at most 0.0042.
Values may be sent and summed in bfloat16 or wider, within the bound.
A program may use at most 64 MiB of HBM per device.

```python
import jax
import jax.numpy as jnp
from jax import lax

D = 4096
K = 256
ROWS = 262144


def plant(entries, stream_key, smallest, top_value):
    place = [jax.random.randint(jax.random.fold_in(stream_key, axis), (), 0, length) for axis, length in enumerate(entries.shape)]
    longest = entries.shape.index(max(entries.shape))
    beside = place[:longest] + [(place[longest] + 1) % entries.shape[longest]] + place[longest + 1:]
    return entries.at[tuple(place)].set(smallest).at[tuple(beside)].set(top_value)


def with_spikes(values, key, source, target, parts, factor):
    owner, partner = [(jnp.arange(values.shape[dim]) // (values.shape[dim] // parts)).reshape([-1 if axis == dim else 1 for axis in range(values.ndim)]) for dim in (source, target)]
    chosen = jax.random.permutation(key, parts)[partner]
    strong = (owner == chosen) | (owner == (partner + parts // 2) % parts)
    return jnp.where(strong, factor * values, values)


def levels(stream_key, shape, shards, smallest, high):
    factor_of, own = 1.0, jax.random.fold_in(stream_key, 6)
    for position, blocks in shards:
        steps = jnp.exp(jax.random.uniform(jax.random.fold_in(own, position), (blocks,), jnp.float32, smallest / len(shards), high / len(shards)))
        factor_of = factor_of * jnp.repeat(steps, shape[position] // blocks).reshape([-1 if axis == position else 1 for axis in range(len(shape))])
    return factor_of


def normal_values(stream_key, extent, width, most, shards=(), held_as=jnp.bfloat16):
    level = levels(stream_key, extent, shards, -0.22, 0.18) if shards else 1.0
    result = jax.random.normal(stream_key, extent, jnp.float32) * width * level
    return jnp.minimum(jnp.maximum(result, -most), most).astype(held_as)


def noise_with(key, shape, spread, most, split, heavy, kind=jnp.bfloat16):
    array = spread * jax.random.normal(key, shape, jnp.float32)
    if split:
        array = array * levels(key, shape, split, -0.22, 0.18)
    return jnp.clip(with_spikes(array, jax.random.fold_in(key, 3), *heavy), -most, most).astype(kind)


def setup_inputs(seed: int = 0) -> dict:
    key_of = jax.random.split(jax.random.key(seed), 5)
    acts = noise_with(key_of[0], (ROWS, D), 1.0, 16.0, ((0, 64), (1, 4)), (0, 1, 64, 4.0))
    basis = normal_values(key_of[1], (D, K), D ** -0.5, 0.09375, ((0, 4),))
    center = normal_values(key_of[2], (D,), 1.0, 6.0, ((0, 4),), jnp.float32)
    mask = plant((jax.random.randint(key_of[3], (ROWS,), 0, 4) < 3).astype(jnp.int32), jax.random.fold_in(key_of[3], 1), 0, 1)
    return {"acts": acts, "basis": basis, "center": center, "mask": mask}


def reference(acts, basis, center, mask):
    high = lax.Precision.HIGHEST
    projected = jnp.dot(acts.astype(jnp.float32), basis.astype(jnp.float32), preferred_element_type=jnp.float32).astype(jnp.bfloat16)
    crossed = lax.dot_general(acts.astype(jnp.float32), projected.astype(jnp.float32), (((0,), (0,)), ((), ())), preferred_element_type=jnp.float32)
    crossed = crossed / jnp.float32(ROWS) + basis.astype(jnp.float32)
    gram_matrix = jnp.dot(crossed.T, crossed, precision=high)
    factor = jnp.linalg.cholesky(gram_matrix)
    orthonormal = lax.linalg.triangular_solve(factor, crossed, left_side=False, lower=True, transpose_a=True)
    offset = jnp.dot(center, orthonormal, precision=high)
    scores = (jnp.dot(acts.astype(jnp.float32), orthonormal.astype(jnp.bfloat16).astype(jnp.float32), preferred_element_type=jnp.float32) - offset[None, :]).astype(jnp.bfloat16)
    weights = mask.astype(jnp.float32)
    mask_half = mask.astype(jnp.bfloat16)
    weight_sum = jnp.sum(weights)
    first_moment = jnp.dot(mask_half.astype(jnp.float32), scores.astype(jnp.float32), preferred_element_type=jnp.float32)
    second_moment = lax.dot_general((scores * mask_half[:, None]).astype(jnp.float32), scores.astype(jnp.float32), (((0,), (0,)), ((), ())), preferred_element_type=jnp.float32)
    subset_mean = first_moment / jnp.maximum(weight_sum, 1.0)
    subset_cov = (second_moment - weight_sum * jnp.outer(subset_mean, subset_mean)) / jnp.maximum(weight_sum - 1.0, 1.0)
    return (orthonormal, scores, subset_mean, subset_cov)
```

```python
import functools

import jax
import jax.numpy as jnp
from jax import lax
from jax.experimental import pallas as pl
from jax.experimental.pallas import tpu as pltpu
from jax.sharding import PartitionSpec as P

MESH = pl.DeviceIdType.MESH
F32 = jnp.float32
BF16 = jnp.bfloat16
CHUNK = 256
NZ, NY, NXH = 8, 4, 2
ROW_CONTRACT = (((0,), (0,)), ((), ()))
LANE_CONTRACT = (((1,), (1,)), ((), ()))
PLAIN = (((1,), (0,)), ((), ()))


def where_am_i():
    r = lax.axis_index("rows")
    p = lax.axis_index("panel")
    z, y, xh = lax.div(r, NY * NXH), lax.rem(lax.div(r, NXH), NY), lax.rem(r, NXH)
    return z, y, xh, lax.div(p, 2), lax.rem(p, 2)


def device(z, y, xh, xl, core):
    return (z * (NY * NXH) + y * NXH + xh, xl * 2 + core)


def remote(src, dst, send_sem, recv_sem, dev):
    return pltpu.make_async_remote_copy(
        src_ref=src, dst_ref=dst, send_sem=send_sem, recv_sem=recv_sem, device_id=dev, device_id_type=MESH
    )


def loop(count, start=0):
    def run(body):
        lax.fori_loop(start, count, lambda i, c: (body(i), c)[1], 0)

    return run


def rows_of(block, size):
    return pl.ds(pl.multiple_of(block * size, size), size)


LEAF = 64


def leaf_inverse(a):
    n = a.shape[0]
    tiles = n // 8
    lane = lax.broadcasted_iota(jnp.int32, (n, n), 1)
    row = lax.broadcasted_iota(jnp.int32, (n, n), 0)
    whole = jnp.concatenate([a, jnp.where(lane == row, 1.0, 0.0)], axis=1)
    m = [whole[8 * t : 8 * t + 8, :] for t in range(tiles)]
    shape = m[0].shape
    sub = lax.broadcasted_iota(jnp.int32, shape, 0)
    out = []
    for t0 in range(tiles):
        diag = jnp.ones(shape, F32)
        cols = [
            [jnp.broadcast_to(m[t][:, k : k + 1], shape) for t in range(t0, tiles)]
            for k in range(8 * t0, 8 * t0 + 8)
        ]
        for s in range(8):
            pivot = jnp.broadcast_to(cols[s][0][s : s + 1, :], shape)
            diag = jnp.where(sub == s, pivot, diag)
            inverse = 1.0 / pivot
            prow = jnp.broadcast_to(m[t0][s : s + 1, :], shape)
            heads = [jnp.broadcast_to(cols[c][0][s : s + 1, :], shape) for c in range(s + 1, 8)]
            for t in range(t0, tiles):
                f = cols[s][t - t0] * inverse
                if t == t0:
                    f = jnp.where(sub > s, f, 0.0)
                m[t] = m[t] - f * prow
                for c in range(s + 1, 8):
                    cols[c][t - t0] = cols[c][t - t0] - f * heads[c - s - 1]
        r = lax.rsqrt(diag)
        r = r * (1.5 - 0.5 * diag * r * r)
        out.append(m[t0] * r)
    return jnp.concatenate(out, axis=0)[:, n:]


def dot32(a, b, dims):
    return lax.dot_general(a, b, dims, precision=lax.Precision.HIGHEST, preferred_element_type=F32)


def factor_inverse(a):
    n = a.shape[0]
    if n == LEAF:
        return leaf_inverse(a)
    h = n // 2
    w11 = factor_inverse(a[:h, :h])
    l21 = dot32(a[h:, :h], w11, LANE_CONTRACT)
    w22 = factor_inverse(a[h:, h:] - dot32(l21, l21, LANE_CONTRACT))
    w21 = -dot32(dot32(w22, l21, PLAIN), w11, PLAIN)
    upper = jnp.concatenate([w11, jnp.zeros((h, h), F32)], axis=1)
    return jnp.concatenate([upper, jnp.concatenate([w21, w22], axis=1)], axis=0)


def ortho_kernel(gram_ref, hi_ref, lo_ref, ortho_ref, half_ref):
    inverse = factor_inverse(gram_ref[...])
    w_hi = inverse.astype(BF16)
    w_lo = (inverse - w_hi.astype(F32)).astype(BF16)
    dims = (((0,), (1,)), ((), ()))
    for j in range(NY):
        hi, lo = hi_ref[j], lo_ref[j]
        q = lax.dot_general(hi, w_lo, dims, preferred_element_type=F32)
        q += lax.dot_general(lo, w_hi, dims, preferred_element_type=F32)
        q += lax.dot_general(hi, w_hi, dims, preferred_element_type=F32)
        ortho_ref[j * 256 : (j + 1) * 256, :] = q
        half_ref[j * 256 : (j + 1) * 256, :] = q.astype(BF16)


def ortho_call(gram, hi, lo):
    k = gram.shape[0]
    cols = NY * 256
    return pl.pallas_call(
        ortho_kernel,
        out_shape=(jax.ShapeDtypeStruct((cols, k), F32), jax.ShapeDtypeStruct((cols, k), BF16)),
        in_specs=[pl.BlockSpec(memory_space=pltpu.VMEM)] * 3,
        out_specs=(pl.BlockSpec(memory_space=pltpu.VMEM),) * 2,
        name="orthonormalise",
    )(gram, hi, lo)


def cross_kernel(
    rows_total, acts_hbm, basis_ref, hi_ref, lo_ref, gram_ref,
    acts, tosib, fromsib, own, cout, cin, total, acc, ysend, yrecv, s32, zsend, zrecv, bt, ct,
    g, gsib, gx, gc, gtot,
    ld, sib_s, sib_r, c_s, c_r, t_s, t_r, y_s, y_r, z_s, z_r, az_s, az_r, ay_s, ay_r, g_s, g_r,
):
    z, y, xh, xl, core = where_am_i()
    zx = z * NXH + xh
    nzx = NZ * NXH
    chunks = acts.shape[0] // CHUNK // 2
    sibling = device(z, y, xh, xl, 1 - core)
    across = device(z, y, xh, 1 - xl, core)

    def ypeer(d):
        q = lax.rem(y + d, NY)
        return q, device(z, q, xh, xl, core)

    def zpeer(d):
        q = lax.rem(zx + d, nzx)
        return q, device(lax.div(q, NXH), y, lax.rem(q, NXH), xl, core)

    def load(k):
        at = rows_of(k, CHUNK)
        return pltpu.make_async_copy(acts_hbm.at[at, :], acts.at[at, :], ld.at[k])

    their, mine = (1 - core) * chunks, core * chunks

    @loop(chunks)
    def _(i):
        load(their + i).start()

    @loop(chunks)
    def _(i):
        load(mine + i).start()

    barrier = pltpu.get_barrier_semaphore()
    for dev in (sibling, across):
        pl.semaphore_signal(barrier, inc=1, device_id=dev, device_id_type=MESH)

    @loop(NY, 1)
    def _(d):
        pl.semaphore_signal(barrier, inc=1, device_id=ypeer(d)[1], device_id_type=MESH)

    @loop(nzx, 1)
    def _(d):
        pl.semaphore_signal(barrier, inc=1, device_id=zpeer(d)[1], device_id_type=MESH)

    @loop(chunks)
    def _(i):
        load(their + i).wait()
        tosib[i] = jnp.dot(
            acts[rows_of(their + i, CHUNK), :], basis_ref[...], preferred_element_type=F32
        ).astype(BF16)

    pl.semaphore_wait(barrier, 2 + (NY - 1) + (nzx - 1))

    def sib_copy(i):
        return remote(tosib.at[i], fromsib.at[i], sib_s.at[i], sib_r.at[i], sibling)

    def c_copy(i):
        return remote(cout.at[i], cin.at[i], c_s.at[i], c_r.at[i], across)

    def t_copy(i, half):
        return remote(total.at[half, i], total.at[half, i], t_s.at[i], t_r.at[i], sibling)

    @loop(chunks)
    def _(i):
        sib_copy(i).start()

    @loop(chunks)
    def _(i):
        load(mine + i).wait()
        part = jnp.dot(acts[rows_of(mine + i, CHUNK), :], basis_ref[...], preferred_element_type=F32)
        sib_copy(i).wait_recv()
        part = part + fromsib[i].astype(F32)
        own[i] = part
        cout[i] = part.astype(BF16)
        c_copy(i).start()

    bt[...] = basis_ref[rows_of(y, 256), :].astype(F32).T.reshape(bt.shape)
    acc[...] = jnp.zeros_like(acc)

    def add_terms(tot, k):
        for j in range(NY):
            acc[j] += lax.dot_general(
                tot, acts[rows_of(k, CHUNK), j * 256 : (j + 1) * 256], ROW_CONTRACT, preferred_element_type=F32
            )

    @loop(chunks)
    def _(i):
        c_copy(i).wait_recv()
        tot = (own[i] + cin[i].astype(F32)).astype(BF16)
        total[core, i] = tot
        t_copy(i, core).start()
        add_terms(tot, mine + i)
        t_copy(i, 1 - core).wait_recv()
        add_terms(total[1 - core, i], their + i)

    ysend[...] = acc[...].astype(BF16)

    def y_copy(d):
        q, dev = ypeer(d)
        return remote(ysend.at[q], yrecv.at[d], y_s.at[d], y_r.at[d], dev)

    @loop(NY, 1)
    def _(d):
        y_copy(d).start()

    s32[...] = acc[y].reshape(s32.shape)

    @loop(NY, 1)
    def _(d):
        y_copy(d).wait_recv()
        s32[...] += yrecv[d].astype(F32).reshape(s32.shape)

    zsend[...] = s32[...].astype(BF16)

    def z_copy(d):
        q, dev = zpeer(d)
        return remote(zsend.at[q], zrecv.at[d], z_s.at[d], z_r.at[d], dev)

    @loop(nzx, 1)
    def _(d):
        z_copy(d).start()

    def add_z(d, s):
        z_copy(d).wait_recv()
        return s + zrecv[d].astype(F32)

    block = lax.fori_loop(1, nzx, add_z, s32[zx])
    block = block / F32(rows_total) + bt[zx]
    upper = block.astype(BF16)
    ct[0, y, zx] = upper
    ct[1, y, zx] = (block - upper.astype(F32)).astype(BF16)

    def az_copy(d, part):
        at = ct.at[part, y, zx]
        return remote(at, at, az_s.at[part, d], az_r.at[part, d], zpeer(d)[1])

    def ay_copy(d, part):
        at = ct.at[part, y]
        return remote(at, at, ay_s.at[part, d], ay_r.at[part, d], ypeer(d)[1])

    for part in range(2):

        @loop(nzx, 1)
        def _(d, part=part):
            az_copy(d, part).start()

    for part in range(2):

        @loop(nzx, 1)
        def _(d, part=part):
            az_copy(d, part).wait_recv()

        @loop(NY, 1)
        def _(d, part=part):
            ay_copy(d, part).start()

    @loop(NY, 1)
    def _(d):
        ay_copy(d, 0).wait_recv()

    gram = jnp.zeros((256, 256), F32)
    for j in range(NY):
        piece = ct[0, j].reshape(256, 256)
        gram += lax.dot_general(piece, piece, LANE_CONTRACT, preferred_element_type=F32)
    g[...] = gram.reshape(g.shape)
    first = remote(g, gsib, g_s.at[0], g_r.at[0], sibling)
    first.start()
    hi_ref[...] = ct[0].reshape(hi_ref.shape)
    first.wait_recv()
    gx[...] = g[...] + gsib[...]
    second = remote(gx.at[core], gc, g_s.at[1], g_r.at[1], across)
    second.start()
    second.wait_recv()
    gtot[core] = gx[core] + gc[...]
    third = remote(gtot.at[core], gtot.at[core], g_s.at[2], g_r.at[2], sibling)
    third.start()
    third.wait_recv()
    gram_ref[...] = gtot[...].reshape(256, 256)

    @loop(NY, 1)
    def _(d):
        ay_copy(d, 1).wait_recv()

    lo_ref[...] = ct[1].reshape(lo_ref.shape)

    @loop(chunks)
    def _(i):
        sib_copy(i).wait_send()
        c_copy(i).wait_send()
        t_copy(i, core).wait_send()

    @loop(NY, 1)
    def _(d):
        y_copy(d).wait_send()
        ay_copy(d, 0).wait_send()
        ay_copy(d, 1).wait_send()

    @loop(nzx, 1)
    def _(d):
        z_copy(d).wait_send()
        az_copy(d, 0).wait_send()
        az_copy(d, 1).wait_send()

    first.wait_send()
    second.wait_send()
    third.wait_send()


def cross_call(acts, basis, rows_total):
    rows, cols = acts.shape
    k = basis.shape[1]
    chunks = rows // CHUNK // 2
    nzx = NZ * NXH
    dma = pltpu.SemaphoreType.DMA
    vm = pltpu.VMEM
    return pl.pallas_call(
        functools.partial(cross_kernel, rows_total),
        out_shape=(jax.ShapeDtypeStruct((NY, k, 256), BF16),) * 2 + (jax.ShapeDtypeStruct((k, k), F32),),
        in_specs=[pl.BlockSpec(memory_space=pl.ANY), pl.BlockSpec(memory_space=vm)],
        out_specs=(pl.BlockSpec(memory_space=vm),) * 3,
        scratch_shapes=[
            vm((rows, cols), BF16),
            vm((chunks, CHUNK, k), BF16),
            vm((chunks, CHUNK, k), BF16),
            vm((chunks, CHUNK, k), F32),
            vm((chunks, CHUNK, k), BF16),
            vm((chunks, CHUNK, k), BF16),
            vm((2, chunks, CHUNK, k), BF16),
            vm((NY, k, 256), F32),
            vm((NY, k, 256), BF16),
            vm((NY, k, 256), BF16),
            vm((nzx, k // nzx, 256), F32),
            vm((nzx, k // nzx, 256), BF16),
            vm((nzx, k // nzx, 256), BF16),
            vm((nzx, k // nzx, 256), F32),
            vm((2, NY, nzx, k // nzx, 256), BF16),
            vm((2, k // 2, k), F32),
            vm((2, k // 2, k), F32),
            vm((2, k // 2, k), F32),
            vm((k // 2, k), F32),
            vm((2, k // 2, k), F32),
            dma((2 * chunks,)),
        ]
        + [dma((chunks,))] * 6
        + [dma((NY,))] * 2
        + [dma((nzx,))] * 2
        + [dma((2, nzx))] * 2
        + [dma((2, NY))] * 2
        + [dma((3,))] * 2,
        compiler_params=pltpu.CompilerParams(collective_id=0, has_side_effects=True),
        name="cross_terms",
    )(acts, basis)


def score_kernel(
    acts_hbm, ortho_ref, offset_ref, mask_ref, scores_ref, mean_ref, cov_ref,
    acts, tosib, fromsib, cout, cin, mine, sc, mom, mrecv, hsum, xrecv, zbuf, fin,
    ld, sib_s, sib_r, c_s, c_r, m_s, m_r, x_s, x_r, zz_s, zz_r, ax_s, ax_r,
):
    z, y, xh, xl, core = where_am_i()
    x = xh * 2 + xl
    xy = x * NY + y
    nxy = 4 * NY
    quarter = acts.shape[0] // 4
    chunks = quarter // CHUNK
    sibling = device(z, y, xh, xl, 1 - core)
    across = device(z, y, xh, 1 - xl, core)

    def xypeer(d):
        q = lax.rem(xy + d, nxy)
        px = lax.div(q, NY)
        return q, device(z, lax.rem(q, NY), lax.div(px, 2), lax.rem(px, 2), core)

    def zpeer(d):
        return device(lax.rem(z + d, NZ), y, xh, xl, core)

    def load(k):
        at = rows_of(k, CHUNK)
        return pltpu.make_async_copy(acts_hbm.at[at, :], acts.at[at, :], ld.at[k])

    def first_chunk(there, c):
        return ((xl + there - 2 * xl * there) * 2 + c) * chunks

    order = [(1, 1 - core, 0), (0, 1 - core, 1), (1, core, 0), (0, core, 1)]
    for there, c, _ in order:

        @loop(chunks)
        def _(i, there=there, c=c):
            load(first_chunk(there, c) + i).start()

    barrier = pltpu.get_barrier_semaphore()
    pl.semaphore_signal(barrier, inc=1, device_id=sibling, device_id_type=MESH)

    @loop(nxy, 1)
    def _(d):
        pl.semaphore_signal(barrier, inc=1, device_id=xypeer(d)[1], device_id_type=MESH)

    @loop(NZ, 1)
    def _(d):
        pl.semaphore_signal(barrier, inc=1, device_id=zpeer(d), device_id_type=MESH)

    def part_of(k):
        load(k).wait()
        return jnp.dot(acts[rows_of(k, CHUNK), :], ortho_ref[...], preferred_element_type=F32) - offset_ref[...]

    for there, slot in ((1, 0), (0, 1)):

        @loop(chunks)
        def _(i, there=there, slot=slot):
            tosib[slot, i] = part_of(first_chunk(there, 1 - core) + i).astype(BF16)

    pl.semaphore_wait(barrier, 1 + (nxy - 1) + (NZ - 1))

    def sib_copy(slot, i):
        return remote(tosib.at[slot, i], fromsib.at[slot, i], sib_s.at[slot, i], sib_r.at[slot, i], sibling)

    def c_copy(i):
        return remote(cout.at[i], cin.at[i], c_s.at[i], c_r.at[i], across)

    for slot in range(2):

        @loop(chunks)
        def _(i, slot=slot):
            sib_copy(slot, i).start()

    @loop(chunks)
    def _(i):
        part = part_of(first_chunk(1, core) + i)
        sib_copy(0, i).wait_recv()
        cout[i] = (part + fromsib[0, i].astype(F32)).astype(BF16)
        c_copy(i).start()

    @loop(chunks)
    def _(i):
        part = part_of(first_chunk(0, core) + i)
        sib_copy(1, i).wait_recv()
        mine[i] = part + fromsib[1, i].astype(F32)

    second = jnp.zeros((256, 256), F32)
    first = jnp.zeros((256, 128), F32)
    ones = jnp.ones((CHUNK, 128), BF16)
    base = pl.multiple_of((xl * 2 + core) * quarter, quarter)
    for i in range(chunks):
        c_copy(i).wait_recv()
        score = (mine[i] + cin[i].astype(F32)).astype(BF16)
        sc[i] = score
        weight = mask_ref[:, pl.ds(pl.multiple_of(base + i * CHUNK, CHUNK), CHUNK)].astype(F32)
        chosen = (score.astype(F32).T * weight).astype(BF16)
        second += jnp.dot(chosen, score, preferred_element_type=F32)
        first += jnp.dot(chosen, ones, preferred_element_type=F32)
    count = jnp.sum(mask_ref[:, pl.ds(base, quarter)].astype(F32), keepdims=True)
    lane = lax.broadcasted_iota(jnp.int32, first.shape, 1)
    side = jnp.where(lane == 1, count, first)
    mom[:, :, :, 0:256] = second.reshape(2, nxy, 8, 256)
    mom[:, :, :, 256:384] = side.reshape(2, nxy, 8, 128)
    scores_ref[...] = sc[...].reshape(scores_ref.shape)

    halves = remote(mom.at[1 - core], mrecv, m_s.at[0], m_r.at[0], sibling)
    halves.start()
    halves.wait_recv()
    hsum[...] = mom[core] + mrecv[...]

    def x_copy(d):
        q, dev = xypeer(d)
        return remote(hsum.at[q], xrecv.at[d], x_s.at[d], x_r.at[d], dev)

    @loop(nxy, 1)
    def _(d):
        x_copy(d).start()

    def add_x(d, s):
        x_copy(d).wait_recv()
        return s + xrecv[d]

    zbuf[z] = lax.fori_loop(1, nxy, add_x, hsum[xy])

    def zz_copy(d):
        return remote(zbuf.at[z], zbuf.at[z], zz_s.at[d], zz_r.at[d], zpeer(d))

    @loop(NZ, 1)
    def _(d):
        zz_copy(d).start()

    @loop(NZ, 1)
    def _(d):
        zz_copy(d).wait_recv()

    tot = zbuf[0]
    for d in range(1, NZ):
        tot = tot + zbuf[d]
    fin[core, xy] = tot

    def ax_copy(d):
        return remote(fin.at[core, xy], fin.at[core, xy], ax_s.at[d], ax_r.at[d], xypeer(d)[1])

    @loop(nxy, 1)
    def _(d):
        ax_copy(d).start()

    @loop(nxy, 1)
    def _(d):
        ax_copy(d).wait_recv()

    whole = remote(fin.at[core], fin.at[core], m_s.at[1], m_r.at[1], sibling)
    whole.start()
    whole.wait_recv()

    second = fin[:, :, :, 0:256].reshape(256, 256)
    side = fin[:, :, :, 256:384].reshape(256, 128)
    weight_sum = side[0:1, 1:2]
    mean = side / jnp.maximum(weight_sum, 1.0)
    mean_row = mean.T[0:1, :]
    mean_ref[...] = mean_row
    cov_ref[...] = (second - weight_sum * (mean[:, 0:1] * mean_row)) / jnp.maximum(weight_sum - 1.0, 1.0)

    for slot in range(2):

        @loop(chunks)
        def _(i, slot=slot):
            sib_copy(slot, i).wait_send()

    @loop(chunks)
    def _(i):
        c_copy(i).wait_send()

    halves.wait_send()
    whole.wait_send()

    @loop(nxy, 1)
    def _(d):
        x_copy(d).wait_send()
        ax_copy(d).wait_send()

    @loop(NZ, 1)
    def _(d):
        zz_copy(d).wait_send()


def score_call(acts, ortho_half, offset_part, mask):
    rows, cols = acts.shape
    k = ortho_half.shape[1]
    chunks = rows // 4 // CHUNK
    nxy = 4 * NY
    dma = pltpu.SemaphoreType.DMA
    vm = pltpu.VMEM
    return pl.pallas_call(
        score_kernel,
        out_shape=(
            jax.ShapeDtypeStruct((rows // 4, k), BF16),
            jax.ShapeDtypeStruct((1, k), F32),
            jax.ShapeDtypeStruct((k, k), F32),
        ),
        in_specs=[pl.BlockSpec(memory_space=pl.ANY)] + [pl.BlockSpec(memory_space=vm)] * 3,
        out_specs=(pl.BlockSpec(memory_space=vm),) * 3,
        scratch_shapes=[
            vm((rows, cols), BF16),
            vm((2, chunks, CHUNK, k), BF16),
            vm((2, chunks, CHUNK, k), BF16),
            vm((chunks, CHUNK, k), BF16),
            vm((chunks, CHUNK, k), BF16),
            vm((chunks, CHUNK, k), F32),
            vm((chunks, CHUNK, k), BF16),
            vm((2, nxy, 8, k + 128), F32),
            vm((nxy, 8, k + 128), F32),
            vm((nxy, 8, k + 128), F32),
            vm((nxy, 8, k + 128), F32),
            vm((NZ, 8, k + 128), F32),
            vm((2, nxy, 8, k + 128), F32),
            dma((4 * chunks,)),
            dma((2, chunks)),
            dma((2, chunks)),
            dma((chunks,)),
            dma((chunks,)),
            dma((2,)),
            dma((2,)),
            dma((nxy,)),
            dma((nxy,)),
            dma((NZ,)),
            dma((NZ,)),
            dma((nxy,)),
            dma((nxy,)),
        ],
        compiler_params=pltpu.CompilerParams(collective_id=1, has_side_effects=True),
        name="scores_and_moments",
    )(acts, ortho_half, offset_part, mask)


def per_device(acts, basis, center, mask):
    high = lax.Precision.HIGHEST
    rows_total = acts.shape[0] * lax.axis_size("rows")
    hi, lo, gram_matrix = cross_call(acts, basis, rows_total)
    orthonormal, ortho_half = ortho_call(gram_matrix, hi, lo)
    offset_part = jnp.dot(center[None, :], orthonormal, precision=high)
    scores, mean, cov = score_call(acts, ortho_half, offset_part, mask[None, :])
    return (orthonormal, scores, mean.reshape(-1), cov)


def solution(mesh):
    placed = (P("rows", "panel"), P("panel", None), P("panel"), P("rows"))
    return jax.shard_map(
        per_device,
        mesh=mesh,
        in_specs=placed,
        out_specs=(P("panel", None), P(("rows", "panel"), None), P(), P()),
        check_vma=False,
    )
```

```python
import functools

import jax
import jax.numpy as jnp
from jax import lax
from jax.experimental import pallas as pl
from jax.experimental.pallas import tpu as pltpu
from jax.sharding import PartitionSpec as P

MESH = pl.DeviceIdType.MESH
F32 = jnp.float32
BF16 = jnp.bfloat16
CHUNK = 256
NZ, NY, NXH = 8, 4, 2
HALF = 128
ROW_CONTRACT = (((0,), (0,)), ((), ()))
LANE_CONTRACT = (((1,), (1,)), ((), ()))
PLAIN = (((1,), (0,)), ((), ()))


def where_am_i():
    r = lax.axis_index("rows")
    p = lax.axis_index("panel")
    z, y, xh = lax.div(r, NY * NXH), lax.rem(lax.div(r, NXH), NY), lax.rem(r, NXH)
    return z, y, xh, lax.div(p, 2), lax.rem(p, 2)


def device(z, y, xh, xl, core):
    return (z * (NY * NXH) + y * NXH + xh, xl * 2 + core)


def remote(src, dst, send_sem, recv_sem, dev):
    return pltpu.make_async_remote_copy(
        src_ref=src, dst_ref=dst, send_sem=send_sem, recv_sem=recv_sem, device_id=dev, device_id_type=MESH
    )


def loop(count, start=0):
    def run(body):
        lax.fori_loop(start, count, lambda i, c: (body(i), c)[1], 0)

    return run


def rows_of(block, size):
    return pl.ds(pl.multiple_of(block * size, size), size)


LEAF = 64


def leaf_inverse(a):
    n = a.shape[0]
    tiles = n // 8
    lane = lax.broadcasted_iota(jnp.int32, (n, n), 1)
    row = lax.broadcasted_iota(jnp.int32, (n, n), 0)
    whole = jnp.concatenate([a, jnp.where(lane == row, 1.0, 0.0)], axis=1)
    m = [whole[8 * t : 8 * t + 8, :] for t in range(tiles)]
    shape = m[0].shape
    sub = lax.broadcasted_iota(jnp.int32, shape, 0)
    out = []
    for t0 in range(tiles):
        diag = jnp.ones(shape, F32)
        cols = [
            [jnp.broadcast_to(m[t][:, k : k + 1], shape) for t in range(t0, tiles)]
            for k in range(8 * t0, 8 * t0 + 8)
        ]
        for s in range(8):
            pivot = jnp.broadcast_to(cols[s][0][s : s + 1, :], shape)
            diag = jnp.where(sub == s, pivot, diag)
            inverse = 1.0 / pivot
            prow = jnp.broadcast_to(m[t0][s : s + 1, :], shape)
            heads = [jnp.broadcast_to(cols[c][0][s : s + 1, :], shape) for c in range(s + 1, 8)]
            for t in range(t0, tiles):
                f = cols[s][t - t0] * inverse
                if t == t0:
                    f = jnp.where(sub > s, f, 0.0)
                m[t] = m[t] - f * prow
                for c in range(s + 1, 8):
                    cols[c][t - t0] = cols[c][t - t0] - f * heads[c - s - 1]
        r = lax.rsqrt(diag)
        r = r * (1.5 - 0.5 * diag * r * r)
        out.append(m[t0] * r)
    return jnp.concatenate(out, axis=0)[:, n:]


def dot32(a, b, dims):
    return lax.dot_general(a, b, dims, precision=lax.Precision.HIGHEST, preferred_element_type=F32)


def factor_inverse(a):
    n = a.shape[0]
    if n == LEAF:
        return leaf_inverse(a)
    h = n // 2
    w11 = factor_inverse(a[:h, :h])
    l21 = dot32(a[h:, :h], w11, LANE_CONTRACT)
    w22 = factor_inverse(a[h:, h:] - dot32(l21, l21, LANE_CONTRACT))
    w21 = -dot32(dot32(w22, l21, PLAIN), w11, PLAIN)
    upper = jnp.concatenate([w11, jnp.zeros((h, h), F32)], axis=1)
    return jnp.concatenate([upper, jnp.concatenate([w21, w22], axis=1)], axis=0)


def step_kernel(
    rows_total, acts_hbm, basis_ref, center_ref, mask_ref, ortho_ref, scores_ref, moments_ref,
    acts, tosib, fromsib, own, cout, cin, total, acc, ysend, yrecv, s32, zsend, zrecv, bt, ct,
    g, gsib, gx, gc, gtot, qb, ptosib, pfromsib, pout, pin, mine32, mom, mrecv, hsum, xrecv, zbuf, fin,
    ld, sib_s, sib_r, c_s, c_r, t_s, t_r, y_s, y_r, z_s, z_r, az_s, az_r, ay_s, ay_r, g_s, g_r,
    p_s, p_r, pc_s, pc_r, m_s, m_r, x_s, x_r, zz_s, zz_r, ax_s, ax_r,
):
    z, y, xh, xl, core = where_am_i()
    zx = xh * NZ + z
    nzx = NZ * NXH
    x = xh * 2 + xl
    xy = x * NY + y
    nxy = 4 * NY
    chunks = acts.shape[0] // CHUNK // 2
    quarter = acts.shape[0] // 4
    qchunks = quarter // CHUNK
    sibling = device(z, y, xh, xl, 1 - core)
    across = device(z, y, xh, 1 - xl, core)

    def ypeer(d):
        q = lax.rem(y + d, NY)
        return q, device(z, q, xh, xl, core)

    def zxpeer(d):
        q = lax.rem(zx + d, nzx)
        return q, device(lax.rem(q, NZ), y, lax.div(q, NZ), xl, core)

    def xypeer(d):
        q = lax.rem(xy + d, nxy)
        px = lax.div(q, NY)
        return q, device(z, lax.rem(q, NY), lax.div(px, 2), lax.rem(px, 2), core)

    def zpeer(d):
        return device(lax.rem(z + d, NZ), y, xh, xl, core)

    def load(k):
        at = rows_of(k, CHUNK)
        return pltpu.make_async_copy(acts_hbm.at[at, :], acts.at[at, :], ld.at[k])

    their, mine = (1 - core) * chunks, core * chunks

    @loop(chunks)
    def _(i):
        load(their + i).start()

    @loop(chunks)
    def _(i):
        load(mine + i).start()

    barrier = pltpu.get_barrier_semaphore()
    pl.semaphore_signal(barrier, inc=1, device_id=sibling, device_id_type=MESH)

    @loop(NY, 1)
    def _(d):
        pl.semaphore_signal(barrier, inc=1, device_id=ypeer(d)[1], device_id_type=MESH)

    @loop(nzx, 1)
    def _(d):
        pl.semaphore_signal(barrier, inc=1, device_id=zxpeer(d)[1], device_id_type=MESH)

    @loop(nxy, 1)
    def _(d):
        pl.semaphore_signal(barrier, inc=1, device_id=xypeer(d)[1], device_id_type=MESH)

    def project(k):
        load(k).wait()
        return jnp.dot(acts[rows_of(k, CHUNK), :], basis_ref[...], preferred_element_type=F32)

    @loop(chunks)
    def _(i):
        tosib[i] = project(their + i).astype(BF16)

    @loop(chunks)
    def _(i):
        own[i] = project(mine + i)

    pl.semaphore_wait(barrier, 1 + (NY - 1) + (nzx - 1) + (nxy - 1))

    def sib_copy(i):
        return remote(tosib.at[i], fromsib.at[i], sib_s.at[i], sib_r.at[i], sibling)

    def c_copy(h, i):
        return remote(cout.at[h, i], cin.at[h, i], c_s.at[h, i], c_r.at[h, i], across)

    def t_copy(h, i, who):
        at = total.at[h, who, i]
        return remote(at, at, t_s.at[h, i], t_r.at[h, i], sibling)

    @loop(chunks)
    def _(i):
        sib_copy(i).start()

    @loop(chunks)
    def _(i):
        sib_copy(i).wait_recv()
        part = own[i] + fromsib[i].astype(F32)
        own[i] = part
        for h in range(2):
            cout[h, i] = part[:, h * HALF : (h + 1) * HALF].astype(BF16)
        c_copy(0, i).start()

    @loop(chunks)
    def _(i):
        c_copy(1, i).start()

    turned = basis_ref[rows_of(y, 256), :].astype(F32).T
    for h in range(2):
        for w in range(NXH):
            bt[h, w * NZ : (w + 1) * NZ] = turned[
                h * HALF : (h + 1) * HALF, w * 128 : (w + 1) * 128
            ].reshape(NZ, 16, 128)
    acc[...] = jnp.zeros_like(acc)

    def add_terms(h, tot, k):
        for j in range(NY):
            acc[h, j] += lax.dot_general(
                tot, acts[rows_of(k, CHUNK), j * 256 : (j + 1) * 256], ROW_CONTRACT, preferred_element_type=F32
            )

    def take(h, i):
        c_copy(h, i).wait_recv()
        tot = (own[i, :, h * HALF : (h + 1) * HALF] + cin[h, i].astype(F32)).astype(BF16)
        total[h, core, i] = tot
        t_copy(h, i, core).start()
        add_terms(h, tot, mine + i)
        t_copy(h, i, 1 - core).wait_recv()
        add_terms(h, total[h, 1 - core, i], their + i)

    def y_copy(h, d):
        q, dev = ypeer(d)
        return remote(ysend.at[h, q], yrecv.at[h, d], y_s.at[h, d], y_r.at[h, d], dev)

    def z_copy(h, d):
        q, dev = zxpeer(d)
        return remote(zsend.at[h, q], zrecv.at[h, d], z_s.at[h, d], z_r.at[h, d], dev)

    def az_copy(h, part, d):
        at = ct.at[part, h, y, zx]
        return remote(at, at, az_s.at[part, h, d], az_r.at[part, h, d], zxpeer(d)[1])

    def ay_copy(h, part, d):
        at = ct.at[part, h, y]
        return remote(at, at, ay_s.at[part, h, d], ay_r.at[part, h, d], ypeer(d)[1])

    def scatter_y(h):
        ysend[h] = acc[h].astype(BF16)

        @loop(NY, 1)
        def _(d):
            y_copy(h, d).start()

    def scatter_zx(h):
        s = acc[h, y]
        for d in range(1, NY):
            y_copy(h, d).wait_recv()
            s = s + yrecv[h, d].astype(F32)
        for w in range(NXH):
            s32[h, w * NZ : (w + 1) * NZ] = s[:, w * 128 : (w + 1) * 128].reshape(NZ, 16, 128)
        zsend[h] = s32[h].astype(BF16)

        @loop(nzx, 1)
        def _(d):
            z_copy(h, d).start()

    def gather_zx(h):
        def add_z(d, s):
            z_copy(h, d).wait_recv()
            return s + zrecv[h, d].astype(F32)

        block = lax.fori_loop(1, nzx, add_z, s32[h, zx]) / F32(rows_total) + bt[h, zx]
        upper = block.astype(BF16)
        ct[0, h, y, zx] = upper
        ct[1, h, y, zx] = (block - upper.astype(F32)).astype(BF16)
        for part in range(2):

            @loop(nzx, 1)
            def _(d, part=part):
                az_copy(h, part, d).start()

    def gather_y(h, part):
        @loop(nzx, 1)
        def _(d):
            az_copy(h, part, d).wait_recv()

        @loop(NY, 1)
        def _(d):
            ay_copy(h, part, d).start()

    def gathered(h, part):
        @loop(NY, 1)
        def _(d):
            ay_copy(h, part, d).wait_recv()

    loop(chunks)(lambda i: take(0, i))
    scatter_y(0)
    loop(chunks // 2 + 1)(lambda i: take(1, i))
    scatter_zx(0)
    loop(chunks, chunks // 2 + 1)(lambda i: take(1, i))
    scatter_y(1)
    gather_zx(0)
    scatter_zx(1)
    gather_y(0, 0)
    gather_y(0, 1)
    gather_zx(1)
    gather_y(1, 0)
    gather_y(1, 1)
    gathered(0, 0)
    gathered(1, 0)

    def piece(part, j):
        rows = []
        for h in range(2):
            both = ct[part, h, j]
            rows.append(
                jnp.concatenate([both[w * NZ : (w + 1) * NZ].reshape(HALF, 128) for w in range(NXH)], axis=1)
            )
        return jnp.concatenate(rows, axis=0)

    gram = jnp.zeros((256, 256), F32)
    for j in range(NY):
        high = piece(0, j)
        gram += lax.dot_general(high, high, LANE_CONTRACT, preferred_element_type=F32)
    g[...] = gram.reshape(g.shape)
    first = remote(g, gsib, g_s.at[0], g_r.at[0], sibling)
    first.start()
    first.wait_recv()
    gx[...] = g[...] + gsib[...]
    second = remote(gx.at[core], gc, g_s.at[1], g_r.at[1], across)
    second.start()
    gathered(0, 1)
    gathered(1, 1)
    weighted = jnp.zeros((256, 128), F32)
    for j in range(NY):
        full = piece(0, j).astype(F32) + piece(1, j).astype(F32)
        for w in range(2):
            at = j * 256 + w * 128
            weighted += full[:, w * 128 : (w + 1) * 128] * center_ref[:, at : at + 128]
    seen = jnp.sum(weighted, axis=1, keepdims=True)
    second.wait_recv()
    gtot[core] = gx[core] + gc[...]
    third = remote(gtot.at[core], gtot.at[core], g_s.at[2], g_r.at[2], sibling)
    third.start()
    third.wait_recv()

    inverse = factor_inverse(gtot[...].reshape(256, 256))
    w_hi = inverse.astype(BF16)
    w_lo = (inverse - w_hi.astype(F32)).astype(BF16)
    dims = (((0,), (1,)), ((), ()))
    for j in range(NY):
        high, low = piece(0, j), piece(1, j)
        q = lax.dot_general(high, w_lo, dims, preferred_element_type=F32)
        q += lax.dot_general(low, w_hi, dims, preferred_element_type=F32)
        q += lax.dot_general(high, w_hi, dims, preferred_element_type=F32)
        ortho_ref[j * 256 : (j + 1) * 256, :] = q
        qb[j * 256 : (j + 1) * 256, :] = q.astype(BF16)
    offset = jnp.sum(inverse.T * seen, axis=0, keepdims=True)

    def first_chunk(there, c):
        return ((xl + there - 2 * xl * there) * 2 + c) * qchunks

    def part_of(k):
        return jnp.dot(acts[rows_of(k, CHUNK), :], qb[...], preferred_element_type=F32) - offset

    def p_copy(slot, i):
        return remote(ptosib.at[slot, i], pfromsib.at[slot, i], p_s.at[slot, i], p_r.at[slot, i], sibling)

    def pc_copy(i):
        return remote(pout.at[i], pin.at[i], pc_s.at[i], pc_r.at[i], across)

    def give(slot, i):
        ptosib[slot, i] = part_of(first_chunk(1 - slot, 1 - core) + i)
        p_copy(slot, i).start()

    loop(qchunks)(lambda i: give(0, i))

    @loop(qchunks)
    def _(i):
        part = part_of(first_chunk(1, core) + i)
        p_copy(0, i).wait_recv()
        pout[i] = (part + pfromsib[0, i]).astype(BF16)
        pc_copy(i).start()

    loop(qchunks)(lambda i: give(1, i))

    @loop(qchunks)
    def _(i):
        part = part_of(first_chunk(0, core) + i)
        p_copy(1, i).wait_recv()
        mine32[i] = part + pfromsib[1, i]

    second_moment = jnp.zeros((256, 256), F32)
    first_moment = jnp.zeros((256, 128), F32)
    ones = jnp.ones((CHUNK, 128), BF16)
    base = pl.multiple_of((xl * 2 + core) * quarter, quarter)
    count = jnp.sum(mask_ref[:, pl.ds(base, quarter)].astype(F32), keepdims=True)
    for i in range(qchunks):
        pc_copy(i).wait_recv()
        score = (mine32[i] + pin[i].astype(F32)).astype(BF16)
        scores_ref[i * CHUNK : (i + 1) * CHUNK, :] = score
        weight = mask_ref[:, pl.ds(pl.multiple_of(base + i * CHUNK, CHUNK), CHUNK)].astype(F32)
        chosen = (score.astype(F32).T * weight).astype(BF16)
        second_moment += jnp.dot(chosen, score, preferred_element_type=F32)
        first_moment += jnp.dot(chosen, ones, preferred_element_type=F32)
    lane = lax.broadcasted_iota(jnp.int32, first_moment.shape, 1)
    mom[:, :, :, 0:256] = second_moment.reshape(2, nxy, 8, 256)
    mom[:, :, :, 256:384] = jnp.where(lane == 1, count, first_moment).reshape(2, nxy, 8, 128)

    halves = remote(mom.at[1 - core], mrecv, m_s.at[0], m_r.at[0], sibling)
    halves.start()
    halves.wait_recv()
    hsum[...] = mom[core] + mrecv[...]

    def x_copy(d):
        q, dev = xypeer(d)
        return remote(hsum.at[q], xrecv.at[d], x_s.at[d], x_r.at[d], dev)

    @loop(nxy, 1)
    def _(d):
        x_copy(d).start()

    def add_x(d, s):
        x_copy(d).wait_recv()
        return s + xrecv[d]

    zbuf[z] = lax.fori_loop(1, nxy, add_x, hsum[xy])

    def zz_copy(d):
        return remote(zbuf.at[z], zbuf.at[z], zz_s.at[d], zz_r.at[d], zpeer(d))

    @loop(NZ, 1)
    def _(d):
        zz_copy(d).start()

    @loop(NZ, 1)
    def _(d):
        zz_copy(d).wait_recv()

    tot = zbuf[0]
    for d in range(1, NZ):
        tot = tot + zbuf[d]
    fin[core, xy] = tot

    def ax_copy(d):
        return remote(fin.at[core, xy], fin.at[core, xy], ax_s.at[d], ax_r.at[d], xypeer(d)[1])

    @loop(nxy, 1)
    def _(d):
        ax_copy(d).start()

    @loop(nxy, 1)
    def _(d):
        ax_copy(d).wait_recv()

    whole = remote(fin.at[core], fin.at[core], m_s.at[1], m_r.at[1], sibling)
    whole.start()
    whole.wait_recv()
    moments_ref[...] = fin[...].reshape(moments_ref.shape)

    @loop(chunks)
    def _(i):
        sib_copy(i).wait_send()
        for h in range(2):
            c_copy(h, i).wait_send()
            t_copy(h, i, core).wait_send()

    @loop(NY, 1)
    def _(d):
        for h in range(2):
            y_copy(h, d).wait_send()
            for part in range(2):
                ay_copy(h, part, d).wait_send()

    @loop(nzx, 1)
    def _(d):
        for h in range(2):
            z_copy(h, d).wait_send()
            for part in range(2):
                az_copy(h, part, d).wait_send()

    @loop(qchunks)
    def _(i):
        for slot in range(2):
            p_copy(slot, i).wait_send()
        pc_copy(i).wait_send()

    @loop(nxy, 1)
    def _(d):
        x_copy(d).wait_send()
        ax_copy(d).wait_send()

    @loop(NZ, 1)
    def _(d):
        zz_copy(d).wait_send()

    for copy in (first, second, third, halves, whole):
        copy.wait_send()


def step_call(acts, basis, center, mask, rows_total):
    rows, cols = acts.shape
    k = basis.shape[1]
    chunks = rows // CHUNK // 2
    qchunks = rows // CHUNK // 4
    nzx = NZ * NXH
    nxy = 4 * NY
    wide = k + 128
    dma = pltpu.SemaphoreType.DMA
    vm = pltpu.VMEM
    half = (2, k // 2, k)
    return pl.pallas_call(
        functools.partial(step_kernel, rows_total),
        out_shape=(
            jax.ShapeDtypeStruct((cols, k), F32),
            jax.ShapeDtypeStruct((rows // 4, k), BF16),
            jax.ShapeDtypeStruct((k, wide), F32),
        ),
        in_specs=[pl.BlockSpec(memory_space=pl.ANY)] + [pl.BlockSpec(memory_space=vm)] * 3,
        out_specs=(pl.BlockSpec(memory_space=vm),) * 3,
        scratch_shapes=[
            vm((rows, cols), BF16),
            vm((chunks, CHUNK, k), BF16),
            vm((chunks, CHUNK, k), BF16),
            vm((chunks, CHUNK, k), F32),
            vm((2, chunks, CHUNK, HALF), BF16),
            vm((2, chunks, CHUNK, HALF), BF16),
            vm((2, 2, chunks, CHUNK, HALF), BF16),
            vm((2, NY, HALF, 256), F32),
            vm((2, NY, HALF, 256), BF16),
            vm((2, NY, HALF, 256), BF16),
            vm((2, nzx, 16, 128), F32),
            vm((2, nzx, 16, 128), BF16),
            vm((2, nzx, 16, 128), BF16),
            vm((2, nzx, 16, 128), F32),
            vm((2, 2, NY, nzx, 16, 128), BF16),
            vm(half, F32),
            vm(half, F32),
            vm(half, F32),
            vm((k // 2, k), F32),
            vm(half, F32),
            vm((cols, k), BF16),
            vm((2, qchunks, CHUNK, k), F32),
            vm((2, qchunks, CHUNK, k), F32),
            vm((qchunks, CHUNK, k), BF16),
            vm((qchunks, CHUNK, k), BF16),
            vm((qchunks, CHUNK, k), F32),
            vm((2, nxy, 8, wide), F32),
            vm((nxy, 8, wide), F32),
            vm((nxy, 8, wide), F32),
            vm((nxy, 8, wide), F32),
            vm((NZ, 8, wide), F32),
            vm((2, nxy, 8, wide), F32),
            dma((2 * chunks,)),
            dma((chunks,)),
            dma((chunks,)),
        ]
        + [dma((2, chunks))] * 4
        + [dma((2, NY))] * 2
        + [dma((2, nzx))] * 2
        + [dma((2, 2, nzx))] * 2
        + [dma((2, 2, NY))] * 2
        + [dma((3,))] * 2
        + [dma((2, qchunks))] * 2
        + [dma((qchunks,))] * 2
        + [dma((2,))] * 2
        + [dma((nxy,))] * 2
        + [dma((NZ,))] * 2
        + [dma((nxy,))] * 2,
        compiler_params=pltpu.CompilerParams(
            collective_id=0, has_side_effects=True, vmem_limit_bytes=48 * 1024 * 1024
        ),
        name="pca_step",
    )(acts, basis, center, mask)


def finish_kernel(ortho_in, scores_in, moments_ref, ortho_ref, scores_ref, mean_ref, cov_ref):
    ortho_ref[...] = ortho_in[...]
    scores_ref[...] = scores_in[...]
    k = cov_ref.shape[0]
    second = moments_ref[:, 0:k]
    side = moments_ref[:, k : k + 128]
    weight_sum = side[0:1, 1:2]
    mean = side / jnp.maximum(weight_sum, 1.0)
    mean_row = mean.T[0:1, :]
    mean_ref[...] = mean_row
    cov_ref[...] = (second - weight_sum * (mean[:, 0:1] * mean_row)) / jnp.maximum(weight_sum - 1.0, 1.0)


def finish_call(ortho, scores, moments):
    k = ortho.shape[1]
    return pl.pallas_call(
        finish_kernel,
        out_shape=(
            jax.ShapeDtypeStruct(ortho.shape, F32),
            jax.ShapeDtypeStruct(scores.shape, BF16),
            jax.ShapeDtypeStruct((1, k), F32),
            jax.ShapeDtypeStruct((k, k), F32),
        ),
        in_specs=[pl.BlockSpec(memory_space=pltpu.VMEM)] * 3,
        out_specs=(pl.BlockSpec(memory_space=pltpu.VMEM),) * 4,
        compiler_params=pltpu.CompilerParams(vmem_limit_bytes=16 * 1024 * 1024),
        name="finish",
    )(ortho, scores, moments)


def per_device(acts, basis, center, mask):
    rows_total = acts.shape[0] * lax.axis_size("rows")
    moved = step_call(acts, basis, center[None, :], mask[None, :], rows_total)
    orthonormal, scores, mean, cov = finish_call(*moved)
    return (orthonormal, scores, mean.reshape(-1), cov)


def solution(mesh):
    placed = (P("rows", "panel"), P("panel", None), P("panel"), P("rows"))
    return jax.shard_map(
        per_device,
        mesh=mesh,
        in_specs=placed,
        out_specs=(P("panel", None), P(("rows", "panel"), None), P(), P()),
        check_vma=False,
    )
```
